256 devices in a mesh: depth: 64 (over x, z_hi, y), freq: 4 (over z_lo, core).
Axes of the slice: x: 4, y: 4, z: 8 (z_hi: 4, z_lo: 2; z = z_hi * 2 + z_lo), core: 2. Of those that a mesh axis runs over, the one named last changes fastest.
Arguments:
- source_field: float32 [4, 2, 64, 2048], P('freq'), may hold values from -6 to 6
- receiver_data: float32 [4, 2, 64, 2048], P('freq'), may hold values from -6 to 6
- propagator: bfloat16 [4, 64, 16, 6, 2, 128, 128], P('freq', 'depth'), may hold values from -0.102062073 to 0.102062073
- block_columns: int32 [64, 16, 6], P('depth'), may hold values from 0 to 15, as said below
- image_pairs: int32 [64, 8, 2], P('depth'), may hold values from 0 to 15, as said below
Outputs:
- image: float32 [64, 8, 128, 128], P('depth', 'freq')
The draws below stay inside these ranges and needn't reach their ends.
Inputs may be any that keep to these rules, and one draw needn't show every extreme that they name: `block_columns`: each block row lists 6 distinct block columns, its own among them. `image_pairs`: the two block indices of a pair differ by at most one.
All inputs are finite; a program needn't handle non-finite values.
Results may differ from the reference program's by a relative error of at most 0.0003.
Values sent between devices are 32-bit elements; how exact they have to be, the bound alone decides.
A program may use at most 64 MiB of HBM per device.

```python
import math
import jax
import jax.numpy as jnp
from jax import lax

X = 2048
BLOCK = 128
NNZ = 6
NBR = 16
SHOTS = 64
LEVELS = 64
FREQS = 4
NI = 8


def surface_values(key):
    shape = (FREQS, 2, SHOTS, X)
    values = jnp.clip(jax.random.normal(key, shape, jnp.float32), -6.0, 6.0)
    return values.astype(jnp.float32)


def draw_source_field(key, part):
    return surface_values(jax.random.fold_in(key, 21))


def draw_receiver_data(key, part):
    return surface_values(jax.random.fold_in(key, 22))


def draw_propagator(key, part):
    own_key = jax.random.fold_in(key, 23)
    spread = 1.0 / math.sqrt(2.0 * NNZ * BLOCK)
    shape = (FREQS, LEVELS, NBR, NNZ, 2, BLOCK, BLOCK)
    values = jnp.clip(jax.random.normal(own_key, shape, jnp.float32), -4.0, 4.0)
    return (values * spread).astype(jnp.bfloat16)


def draw_block_columns(key, part):
    scores = jax.random.randint(key, (LEVELS, NBR, NBR), 0, 1 << 20)
    columns = jnp.arange(NBR, dtype=jnp.int32)
    scores = scores * NBR + columns[None, None, :]
    diagonal = columns[:, None] == columns[None, :]
    scores = jnp.where(diagonal[None], (1 << 20) * NBR + NBR, scores)
    unused, picked = lax.top_k(scores, NNZ)
    return picked.astype(jnp.int32)


def draw_image_pairs(key, part):
    key_rows = jax.random.fold_in(key, 11)
    key_step = jax.random.fold_in(key, 12)
    key_first = jax.random.fold_in(key, 13)
    key_second = jax.random.fold_in(key, 14)
    block_rows = jax.random.randint(key_rows, (LEVELS, NI), 0, NBR)
    slots = jnp.arange(NI, dtype=jnp.int32)[None, :]
    first_slot = jax.random.randint(key_first, (LEVELS, 1), 0, NI)
    second_slot = (first_slot + 1 + jax.random.randint(key_second, (LEVELS, 1), 0, NI - 1)) % NI
    block_rows = jnp.where(slots == first_slot, 0, jnp.where(slots == second_slot, NBR - 1, block_rows))
    offsets = jax.random.randint(key_step, (LEVELS, NI), -1, 2)
    block_cols = jnp.clip(block_rows + offsets, 0, NBR - 1)
    return jnp.stack([block_rows, block_cols], axis=-1).astype(jnp.int32)


def setup_inputs(seed: int = 0) -> dict:
    arg_keys = jax.random.split(jax.random.key(seed), 6)
    source_field = draw_source_field(jax.random.fold_in(arg_keys[5], 71), 0)
    receiver_data = draw_receiver_data(jax.random.fold_in(arg_keys[5], 71), 0)
    propagator = draw_propagator(jax.random.fold_in(arg_keys[5], 71), 0)
    block_columns = draw_block_columns(jax.random.fold_in(arg_keys[5], 71), 0)
    image_pairs = draw_image_pairs(jax.random.fold_in(arg_keys[5], 71), 0)
    return {"source_field": source_field, "receiver_data": receiver_data, "propagator": propagator, "block_columns": block_columns, "image_pairs": image_pairs}


def edge_taper(lateral):
    position = jnp.arange(lateral, dtype=jnp.int32)
    distance = jnp.minimum(position, lateral - 1 - position).astype(jnp.float32)
    edge_cells = lateral // 32
    edge_ramp = jnp.maximum(0.0, 1.0 - distance / edge_cells)
    return 1.0 - 0.3 * edge_ramp * edge_ramp

def propagate(field, level_operator, level_columns, taper_row):
    lane_count, shot_count, lateral = field.shape
    block_rows = level_columns.shape[0]
    blocks = field.reshape(lane_count, shot_count, block_rows, lateral // block_rows)
    picked = jnp.take(blocks, level_columns, axis=2)
    operator_real = level_operator[:, :, 0].astype(jnp.float32)
    operator_imag = level_operator[:, :, 1].astype(jnp.float32)
    real_part = jnp.einsum('cbrjk,rjkm->cbrm', picked, operator_real, precision=lax.Precision.HIGHEST)
    imag_part = jnp.einsum('cbrjk,rjkm->cbrm', picked, operator_imag, precision=lax.Precision.HIGHEST)
    source_real = real_part[0] - imag_part[1]
    source_imag = real_part[1] + imag_part[0]
    receiver_real = real_part[2] + imag_part[3]
    receiver_imag = real_part[3] - imag_part[2]
    combined = jnp.stack([source_real, source_imag, receiver_real, receiver_imag])
    return combined.reshape(lane_count, shot_count, lateral) * taper_row

def image_level(field, level_pairs):
    lane_count, shot_count, lateral = field.shape
    block_size = lateral // (lateral // BLOCK)
    blocks = field.reshape(lane_count, shot_count, lateral // block_size, block_size)
    source_blocks = jnp.take(blocks[0:2], level_pairs[:, 0], axis=2)
    receiver_blocks = jnp.take(blocks[2:4], level_pairs[:, 1], axis=2)
    return jnp.einsum('csik,csim->ikm', source_blocks, receiver_blocks, precision=lax.Precision.HIGHEST)

def reference(source_field, receiver_data, propagator, block_columns, image_pairs):
    taper_row = edge_taper(X)
    surface = jnp.concatenate([source_field, receiver_data], axis=1).astype(jnp.float32)
    image_scale = 1.0 / math.sqrt(2.0 * SHOTS * FREQS)

    def one_level(wavefield, level_index):
        level_operator = lax.dynamic_index_in_dim(propagator, level_index, 1, keepdims=False)
        level_columns = lax.dynamic_index_in_dim(block_columns, level_index, 0, keepdims=False)
        level_pairs = lax.dynamic_index_in_dim(image_pairs, level_index, 0, keepdims=False)
        advanced = jax.vmap(propagate, in_axes=(0, 0, None, None))(wavefield, level_operator, level_columns, taper_row)
        level_image = lax.optimization_barrier(jnp.sum(jax.vmap(image_level, in_axes=(0, None))(advanced, level_pairs), axis=0))
        return (advanced, level_image * image_scale)
    unused, image = lax.scan(one_level, surface, jnp.arange(LEVELS, dtype=jnp.int32))
    return image
```

```python
import functools
import math

import jax
import jax.numpy as jnp
from jax import lax
from jax.experimental import pallas as pl
from jax.experimental.pallas import tpu as pltpu
from jax.sharding import PartitionSpec as P

GROUP = 2
CHUNK = 2
LANE = 128
MESH = pl.DeviceIdType.MESH


def split(value):
    high = value.astype(jnp.bfloat16)
    low = (value - high.astype(jnp.float32)).astype(jnp.bfloat16)
    return high, low


def edge_row(last_block):
    lane = lax.broadcasted_iota(jnp.int32, (1, LANE), 1)
    distance = LANE - 1 - lane if last_block else lane
    ramp = jnp.maximum(0.0, 1.0 - distance.astype(jnp.float32) / 64.0)
    return 1.0 - 0.3 * ramp * ramp


def kernel(
    levels, bands, scale,
    columns, pairs, source_hbm, receiver_hbm, operator_hbm,
    image,
    operator, surface, incoming, outgoing, pieces, partial, gathered,
    load_sem, send_sem, recv_sem, part_send_sem, part_recv_sem,
):
    level = lax.axis_index("depth")
    band = lax.axis_index("freq")
    following = lax.rem(level + 1, levels)
    preceding = lax.rem(level + levels - 1, levels)
    groups = outgoing.shape[0]
    blocks = outgoing.shape[1]
    rows = outgoing.shape[2]
    half = rows // 2
    nnz = operator.shape[1]
    own_pairs = image.shape[1]

    loads = [
        pltpu.make_async_copy(operator_hbm.at[0, 0], operator, load_sem.at[0]),
        pltpu.make_async_copy(source_hbm.at[0], surface.at[0], load_sem.at[1]),
        pltpu.make_async_copy(receiver_hbm.at[0], surface.at[1], load_sem.at[2]),
    ]
    for load in loads:
        load.start()

    barrier = pltpu.get_barrier_semaphore()
    for target in (following, preceding):
        pl.semaphore_signal(barrier, inc=1, device_id=(target, band), device_id_type=MESH)
    for step in range(1, bands):
        peer = lax.rem(band + step, bands)
        pl.semaphore_signal(barrier, inc=1, device_id=(level, peer), device_id_type=MESH)
    pl.semaphore_wait(barrier, 2 + bands - 1)
    for load in loads:
        load.wait()

    sublane = lax.broadcasted_iota(jnp.int32, (8, LANE), 0)

    @pl.when(level == 0)
    def _():
        def fill(tile, carry):
            shots = pl.ds(pl.multiple_of(tile * 8, 8), 8)
            for block in range(blocks):
                lanes = pl.ds(block * LANE, LANE)
                parts = [
                    surface[0, 0, shots, lanes],
                    surface[1, 0, shots, lanes],
                    surface[0, 1, shots, lanes],
                    surface[1, 1, shots, lanes],
                ]
                for q in range(4):
                    made = parts[0] if q == 0 else pltpu.roll(parts[0], (8 - 2 * q) % 8, 0)
                    for m in range(1, 4):
                        shift = (2 * (m - q)) % 8
                        moved = parts[m] if shift == 0 else pltpu.roll(parts[m], shift, 0)
                        made = jnp.where(sublane >= 2 * m, moved, made)
                    incoming[0, tile * 4 + q, block] = made
            return carry

        lax.fori_loop(0, groups // 4, fill, 0)

    sign = jnp.where((sublane < 2) | (sublane >= 6), -1.0, 1.0).astype(jnp.float32)
    first_edge = edge_row(False)
    last_edge = edge_row(True)
    region = level // (levels - 1)

    def to_next(index, start, size):
        return pltpu.make_async_remote_copy(
            src_ref=outgoing.at[index, pl.ds(start, size)],
            dst_ref=incoming.at[region, index, pl.ds(start, size)],
            send_sem=send_sem,
            recv_sem=recv_sem.at[region, index],
            device_id=(following, band),
            device_id_type=MESH,
        )

    def arrived(which, index):
        pltpu.make_async_copy(
            incoming.at[which, index], incoming.at[which, index], recv_sem.at[which, index]
        ).wait()

    def one_group(index, carry):
        @pl.when(level > 0)
        def _():
            arrived(0, index)

        high, low = split(incoming[0, index])
        pieces[...] = jnp.concatenate([high, low], axis=1)
        for r in range(blocks):
            left = jnp.concatenate([pieces[columns[0, r, j]] for j in range(nnz)], axis=1)
            right = jnp.concatenate(
                [operator[r, :, c].reshape(nnz * LANE, LANE) for c in range(2)], axis=1
            )
            product = jnp.dot(left, right, preferred_element_type=jnp.float32)
            product = product[:rows] + product[rows:]
            turned = pltpu.roll(product[:, LANE:], half, 0)
            value = product[:, :LANE] + sign * turned
            if r == 0:
                value = value * first_edge
            if r == blocks - 1:
                value = value * last_edge
            outgoing[index, r] = value
            if r % CHUNK == CHUNK - 1:
                to_next(index, r + 1 - CHUNK, CHUNK).start()
        return carry

    lax.fori_loop(0, groups, one_group, 0)

    is_source = lax.rem(sublane, 4) < 2
    all_rows = groups * rows

    def one_pair(index, carry):
        left = outgoing[:, pairs[0, index, 0]]
        right = outgoing[:, pairs[0, index, 1]]
        left = jnp.where(is_source[None], left, 0.0)
        right = jnp.concatenate([right[:, 2:], right[:, :2]], axis=1)
        left_high, left_low = split(left.reshape(all_rows, LANE))
        right_high, right_low = split(right.reshape(all_rows, LANE))
        left_all = jnp.concatenate([left_high, left_high, left_low], axis=0)
        right_all = jnp.concatenate([right_high, right_low, right_high], axis=0)
        term = lax.dot_general(
            left_all, right_all, (((0,), (0,)), ((), ())), preferred_element_type=jnp.float32
        )
        partial[index] = term * scale
        return carry

    lax.fori_loop(0, own_pairs * bands, one_pair, 0)

    sends = []
    for step in range(1, bands):
        peer = lax.rem(band + step, bands)
        send = pltpu.make_async_remote_copy(
            src_ref=partial.at[pl.ds(peer * own_pairs, own_pairs)],
            dst_ref=gathered.at[step - 1],
            send_sem=part_send_sem.at[step - 1],
            recv_sem=part_recv_sem.at[step - 1],
            device_id=(level, peer),
            device_id_type=MESH,
        )
        send.start()
        sends.append(send)
    for send in sends:
        send.wait_recv()
    total = partial[pl.ds(band * own_pairs, own_pairs)]
    for step in range(1, bands):
        total = total + gathered[step - 1]
    image[0] = total
    for send in sends:
        send.wait_send()
    pltpu.make_async_copy(outgoing, outgoing, send_sem).wait()

    @pl.when(level == 0)
    def _():
        def drain(index, carry):
            arrived(1, index)
            return carry

        lax.fori_loop(0, groups, drain, 0)


def shards(source_field, receiver_data, propagator, block_columns, image_pairs):
    levels = lax.axis_size("depth")
    bands = lax.axis_size("freq")
    shots, lateral = source_field.shape[2:]
    blocks, nnz = propagator.shape[2:4]
    pair_count = image_pairs.shape[1]
    own_pairs = pair_count // bands
    groups = shots // GROUP
    rows = 4 * GROUP
    scale = 1.0 / math.sqrt(2.0 * shots * bands)
    tile = (LANE, LANE)
    smem = pl.BlockSpec(memory_space=pltpu.SMEM)
    anywhere = pl.BlockSpec(memory_space=pl.ANY)
    return pl.pallas_call(
        functools.partial(kernel, levels, bands, scale),
        out_shape=jax.ShapeDtypeStruct((1, own_pairs) + tile, jnp.float32),
        in_specs=[smem, smem, anywhere, anywhere, anywhere],
        out_specs=pl.BlockSpec(memory_space=pltpu.VMEM),
        scratch_shapes=[
            pltpu.VMEM((blocks, nnz, 2) + tile, jnp.bfloat16),
            pltpu.VMEM((2, 2, shots, lateral), jnp.float32),
            pltpu.VMEM((2, groups, blocks, rows, LANE), jnp.float32),
            pltpu.VMEM((groups, blocks, rows, LANE), jnp.float32),
            pltpu.VMEM((blocks, 2 * rows, LANE), jnp.bfloat16),
            pltpu.VMEM((pair_count,) + tile, jnp.float32),
            pltpu.VMEM((bands - 1, own_pairs) + tile, jnp.float32),
            pltpu.SemaphoreType.DMA((3,)),
            pltpu.SemaphoreType.DMA,
            pltpu.SemaphoreType.DMA((2, groups)),
            pltpu.SemaphoreType.DMA((bands - 1,)),
            pltpu.SemaphoreType.DMA((bands - 1,)),
        ],
        compiler_params=pltpu.CompilerParams(
            collective_id=0, has_side_effects=True, vmem_limit_bytes=48 * 2**20
        ),
    )(block_columns, image_pairs, source_field, receiver_data, propagator)


def solution(mesh):
    placed = (
        P("freq", None, None, None),
        P("freq", None, None, None),
        P("freq", "depth", None, None, None, None, None),
        P("depth", None, None),
        P("depth", None, None),
    )
    return jax.shard_map(
        shards,
        mesh=mesh,
        in_specs=placed,
        out_specs=P("depth", "freq", None, None),
        check_vma=False,
    )
```

```python
import functools
import math

import jax
import jax.numpy as jnp
from jax import lax
from jax.experimental import pallas as pl
from jax.experimental.pallas import tpu as pltpu
from jax.sharding import PartitionSpec as P

GROUP = 2
SPLITS = ((0, 10), (10, 16))
RUN = 4
PLANE = 16
SIDES = 32
LANE = 128
MESH = pl.DeviceIdType.MESH


def split(value):
    high = value.astype(jnp.bfloat16)
    low = (value - high.astype(jnp.float32)).astype(jnp.bfloat16)
    return high, low


def edge_row(last_block):
    lane = lax.broadcasted_iota(jnp.int32, (1, LANE), 1)
    distance = LANE - 1 - lane if last_block else lane
    ramp = jnp.maximum(0.0, 1.0 - distance.astype(jnp.float32) / 64.0)
    return 1.0 - 0.3 * ramp * ramp


def kernel(
    levels, bands, scale,
    columns, pairs, source_hbm, receiver_hbm, operator_hbm,
    image,
    operator, surface, incoming, outgoing, pieces, partial, gathered,
    load_sem, send_sem, relay_sem, recv_sem, part_send_sem, part_recv_sem,
):
    level = lax.axis_index("depth")
    band = lax.axis_index("freq")
    last = level // (levels - 1)
    side_core = lax.rem(band, 2)
    relayed = side_core * (lax.rem(level, RUN) // (RUN - 1)) * (1 - last)
    region = relayed + 2 * last
    detour = PLANE - RUN + 1 + SIDES * (band // 2)
    following = lax.rem(level + 1 + (detour - 1) * relayed, levels)
    following = following + last * (levels - 1)
    next_band = band + last * (1 - 2 * side_core)
    relay_target = lax.rem(level + levels + 1 - detour, levels)
    is_relay = (side_core == 1) & (lax.rem(level, RUN) == 0) & (level != detour - 1)
    groups = outgoing.shape[0]
    blocks = outgoing.shape[1]
    rows = outgoing.shape[2]
    half = rows // 2
    nnz = operator.shape[1]
    own_pairs = image.shape[1]

    loads = [
        pltpu.make_async_copy(operator_hbm.at[0, 0], operator, load_sem.at[0]),
        pltpu.make_async_copy(source_hbm.at[0], surface.at[0], load_sem.at[1]),
        pltpu.make_async_copy(receiver_hbm.at[0], surface.at[1], load_sem.at[2]),
    ]
    for load in loads:
        load.start()

    barrier = pltpu.get_barrier_semaphore()
    distances = [1, detour, detour - 1]
    for distance in distances:
        for step in (distance, levels - distance):
            pl.semaphore_signal(
                barrier,
                inc=1,
                device_id=(lax.rem(level + step, levels), band),
                device_id_type=MESH,
            )
    for step in range(1, bands):
        peer = lax.rem(band + step, bands)
        pl.semaphore_signal(barrier, inc=1, device_id=(level, peer), device_id_type=MESH)
    pl.semaphore_wait(barrier, 2 * len(distances) + bands - 1)
    for load in loads:
        load.wait()

    sublane = lax.broadcasted_iota(jnp.int32, (8, LANE), 0)

    @pl.when(level == 0)
    def _():
        def fill(tile, carry):
            shots = pl.ds(pl.multiple_of(tile * 8, 8), 8)
            for block in range(blocks):
                lanes = pl.ds(block * LANE, LANE)
                parts = [
                    surface[0, 0, shots, lanes],
                    surface[1, 0, shots, lanes],
                    surface[0, 1, shots, lanes],
                    surface[1, 1, shots, lanes],
                ]
                for q in range(4):
                    made = parts[0] if q == 0 else pltpu.roll(parts[0], (8 - 2 * q) % 8, 0)
                    for m in range(1, 4):
                        shift = (2 * (m - q)) % 8
                        moved = parts[m] if shift == 0 else pltpu.roll(parts[m], shift, 0)
                        made = jnp.where(sublane >= 2 * m, moved, made)
                    incoming[0, tile * 4 + q, block] = made
            return carry

        lax.fori_loop(0, groups // 4, fill, 0)

    sign = jnp.where((sublane < 2) | (sublane >= 6), -1.0, 1.0).astype(jnp.float32)
    first_edge = edge_row(False)
    last_edge = edge_row(True)

    def to_next(index, part):
        begin, end = SPLITS[part]
        return pltpu.make_async_remote_copy(
            src_ref=outgoing.at[index, pl.ds(begin, end - begin)],
            dst_ref=incoming.at[region, index, pl.ds(begin, end - begin)],
            send_sem=send_sem,
            recv_sem=recv_sem.at[region, index, part],
            device_id=(following, next_band),
            device_id_type=MESH,
        )

    def arrived(which, index, part):
        begin, end = SPLITS[part]
        landed = incoming.at[which, index, pl.ds(begin, end - begin)]
        pltpu.make_async_copy(landed, landed, recv_sem.at[which, index, part]).wait()

    def pass_on():
        def one(index, carry):
            for part, (begin, end) in enumerate(SPLITS):
                arrived(1, index, part)
                pltpu.make_async_remote_copy(
                    src_ref=incoming.at[1, index, pl.ds(begin, end - begin)],
                    dst_ref=incoming.at[0, index, pl.ds(begin, end - begin)],
                    send_sem=relay_sem,
                    recv_sem=recv_sem.at[0, index, part],
                    device_id=(relay_target, band),
                    device_id_type=MESH,
                ).start()
            return carry

        lax.fori_loop(0, groups, one, 0)
        pltpu.make_async_copy(outgoing, outgoing, relay_sem).wait()

    @pl.when(is_relay & (level >= detour))
    def _():
        pass_on()

    def one_group(index, carry):
        @pl.when(level > 0)
        def _():
            for part in range(len(SPLITS)):
                arrived(0, index, part)

        high, low = split(incoming[0, index])
        pieces[...] = jnp.concatenate([high, low], axis=1)
        for r in range(blocks):
            left = jnp.concatenate([pieces[columns[0, r, j]] for j in range(nnz)], axis=1)
            right = jnp.concatenate(
                [operator[r, :, c].reshape(nnz * LANE, LANE) for c in range(2)], axis=1
            )
            product = jnp.dot(left, right, preferred_element_type=jnp.float32)
            product = product[:rows] + product[rows:]
            turned = pltpu.roll(product[:, LANE:], half, 0)
            value = product[:, :LANE] + sign * turned
            if r == 0:
                value = value * first_edge
            if r == blocks - 1:
                value = value * last_edge
            outgoing[index, r] = value
            for part, (begin, end) in enumerate(SPLITS):
                if r + 1 == end:
                    to_next(index, part).start()
        return carry

    lax.fori_loop(0, groups, one_group, 0)

    is_source = lax.rem(sublane, 4) < 2
    all_rows = groups * rows

    def one_pair(index, carry):
        left = outgoing[:, pairs[0, index, 0]]
        right = outgoing[:, pairs[0, index, 1]]
        left = jnp.where(is_source[None], left, 0.0)
        right = jnp.concatenate([right[:, 2:], right[:, :2]], axis=1)
        left_high, left_low = split(left.reshape(all_rows, LANE))
        right_high, right_low = split(right.reshape(all_rows, LANE))
        left_all = jnp.concatenate([left_high, left_high, left_low], axis=0)
        right_all = jnp.concatenate([right_high, right_low, right_high], axis=0)
        term = lax.dot_general(
            left_all, right_all, (((0,), (0,)), ((), ())), preferred_element_type=jnp.float32
        )
        partial[index] = term * scale
        return carry

    lax.fori_loop(0, own_pairs * bands, one_pair, 0)

    sends = []
    for step in range(1, bands):
        peer = lax.rem(band + step, bands)
        send = pltpu.make_async_remote_copy(
            src_ref=partial.at[pl.ds(peer * own_pairs, own_pairs)],
            dst_ref=gathered.at[step - 1],
            send_sem=part_send_sem.at[step - 1],
            recv_sem=part_recv_sem.at[step - 1],
            device_id=(level, peer),
            device_id_type=MESH,
        )
        send.start()
        sends.append(send)
    for send in sends:
        send.wait_recv()
    total = partial[pl.ds(band * own_pairs, own_pairs)]
    for step in range(1, bands):
        total = total + gathered[step - 1]
    image[0] = total
    for send in sends:
        send.wait_send()
    pltpu.make_async_copy(outgoing, outgoing, send_sem).wait()

    @pl.when(is_relay & (level < detour))
    def _():
        pass_on()

    @pl.when(level == levels - 1)
    def _():
        def drain(index, carry):
            for part in range(len(SPLITS)):
                arrived(2, index, part)
            return carry

        lax.fori_loop(0, groups, drain, 0)


def shards(source_field, receiver_data, propagator, block_columns, image_pairs):
    levels = lax.axis_size("depth")
    bands = lax.axis_size("freq")
    shots, lateral = source_field.shape[2:]
    blocks, nnz = propagator.shape[2:4]
    pair_count = image_pairs.shape[1]
    own_pairs = pair_count // bands
    groups = shots // GROUP
    rows = 4 * GROUP
    scale = 1.0 / math.sqrt(2.0 * shots * bands)
    tile = (LANE, LANE)
    smem = pl.BlockSpec(memory_space=pltpu.SMEM)
    anywhere = pl.BlockSpec(memory_space=pl.ANY)
    return pl.pallas_call(
        functools.partial(kernel, levels, bands, scale),
        out_shape=jax.ShapeDtypeStruct((1, own_pairs) + tile, jnp.float32),
        in_specs=[smem, smem, anywhere, anywhere, anywhere],
        out_specs=pl.BlockSpec(memory_space=pltpu.VMEM),
        scratch_shapes=[
            pltpu.VMEM((blocks, nnz, 2) + tile, jnp.bfloat16),
            pltpu.VMEM((2, 2, shots, lateral), jnp.float32),
            pltpu.VMEM((3, groups, blocks, rows, LANE), jnp.float32),
            pltpu.VMEM((groups, blocks, rows, LANE), jnp.float32),
            pltpu.VMEM((blocks, 2 * rows, LANE), jnp.bfloat16),
            pltpu.VMEM((pair_count,) + tile, jnp.float32),
            pltpu.VMEM((bands - 1, own_pairs) + tile, jnp.float32),
            pltpu.SemaphoreType.DMA((3,)),
            pltpu.SemaphoreType.DMA,
            pltpu.SemaphoreType.DMA,
            pltpu.SemaphoreType.DMA((3, groups, len(SPLITS))),
            pltpu.SemaphoreType.DMA((bands - 1,)),
            pltpu.SemaphoreType.DMA((bands - 1,)),
        ],
        compiler_params=pltpu.CompilerParams(
            collective_id=0, has_side_effects=True, vmem_limit_bytes=48 * 2**20
        ),
    )(block_columns, image_pairs, source_field, receiver_data, propagator)


def solution(mesh):
    placed = (
        P("freq", None, None, None),
        P("freq", None, None, None),
        P("freq", "depth", None, None, None, None, None),
        P("depth", None, None),
        P("depth", None, None),
    )
    return jax.shard_map(
        shards,
        mesh=mesh,
        in_specs=placed,
        out_specs=P("depth", "freq", None, None),
        check_vma=False,
    )
```

```python
import functools
import math

import jax
import jax.numpy as jnp
from jax import lax
from jax.experimental import pallas as pl
from jax.experimental.pallas import tpu as pltpu
from jax.sharding import PartitionSpec as P

GROUP = 2
SPLITS = ((0, 6), (6, 12), (12, 16))
RUN = 4
PLANE = 16
SIDES = 32
LANE = 128
MESH = pl.DeviceIdType.MESH


def split(value):
    high = value.astype(jnp.bfloat16)
    low = (value - high.astype(jnp.float32)).astype(jnp.bfloat16)
    return high, low


def edge_row(last_block):
    lane = lax.broadcasted_iota(jnp.int32, (1, LANE), 1)
    distance = LANE - 1 - lane if last_block else lane
    ramp = jnp.maximum(0.0, 1.0 - distance.astype(jnp.float32) / 64.0)
    return 1.0 - 0.3 * ramp * ramp


def kernel(
    levels, bands, scale,
    columns_hbm, pairs_hbm, source_hbm, receiver_hbm, operator_hbm,
    image,
    columns, pairs, operator, surface, incoming, outgoing, pieces, partial, gathered,
    load_sem, send_sem, relay_sem, recv_sem, part_send_sem, part_recv_sem,
):
    level = lax.axis_index("depth")
    band = lax.axis_index("freq")
    last = level // (levels - 1)
    side_core = lax.rem(band, 2)
    relayed = side_core * (lax.rem(level, RUN) // (RUN - 1)) * (1 - last)
    region = relayed + 2 * last
    detour = PLANE - RUN + 1 + SIDES * (band // 2)
    following = lax.rem(level + 1 + (detour - 1) * relayed, levels)
    following = following + last * (levels - 1)
    next_band = band + last * (1 - 2 * side_core)
    relay_target = lax.rem(level + levels + 1 - detour, levels)
    is_relay = (side_core == 1) & (lax.rem(level, RUN) == 0) & (level != detour - 1)
    groups = outgoing.shape[0]
    blocks = outgoing.shape[1]
    rows = outgoing.shape[2]
    half = rows // 2
    nnz = operator.shape[1]
    own_pairs = image.shape[1]

    loads = [
        pltpu.make_async_copy(source_hbm.at[0], surface.at[0], load_sem.at[0]),
        pltpu.make_async_copy(receiver_hbm.at[0], surface.at[1], load_sem.at[1]),
        pltpu.make_async_copy(operator_hbm.at[0, 0], operator, load_sem.at[2]),
        pltpu.make_async_copy(columns_hbm, columns, load_sem.at[3]),
        pltpu.make_async_copy(pairs_hbm, pairs, load_sem.at[4]),
    ]
    for load in loads:
        load.start()

    barrier = pltpu.get_barrier_semaphore()
    distances = [1, detour, detour - 1]
    for distance in distances:
        for step in (distance, levels - distance):
            pl.semaphore_signal(
                barrier,
                inc=1,
                device_id=(lax.rem(level + step, levels), band),
                device_id_type=MESH,
            )
    for step in range(1, bands):
        peer = lax.rem(band + step, bands)
        pl.semaphore_signal(barrier, inc=1, device_id=(level, peer), device_id_type=MESH)
    pl.semaphore_wait(barrier, 2 * len(distances) + bands - 1)
    for load in loads:
        load.wait()

    sublane = lax.broadcasted_iota(jnp.int32, (8, LANE), 0)

    def fill(tile):
        shots = pl.ds(pl.multiple_of(tile * 8, 8), 8)
        for block in range(blocks):
            lanes = pl.ds(block * LANE, LANE)
            parts = [
                surface[0, 0, shots, lanes],
                surface[1, 0, shots, lanes],
                surface[0, 1, shots, lanes],
                surface[1, 1, shots, lanes],
            ]
            for q in range(4):
                made = parts[0] if q == 0 else pltpu.roll(parts[0], (8 - 2 * q) % 8, 0)
                for m in range(1, 4):
                    shift = (2 * (m - q)) % 8
                    moved = parts[m] if shift == 0 else pltpu.roll(parts[m], shift, 0)
                    made = jnp.where(sublane >= 2 * m, moved, made)
                incoming[0, tile * 4 + q, block] = made

    @pl.when(level == 0)
    def _():
        def one_tile(tile, carry):
            fill(tile)
            return carry

        lax.fori_loop(0, groups // 4, one_tile, 0)

    sign = jnp.where((sublane < 2) | (sublane >= 6), -1.0, 1.0).astype(jnp.float32)
    first_edge = edge_row(False)
    last_edge = edge_row(True)

    def to_next(index, part):
        begin, end = SPLITS[part]
        return pltpu.make_async_remote_copy(
            src_ref=outgoing.at[index, pl.ds(begin, end - begin)],
            dst_ref=incoming.at[region, index, pl.ds(begin, end - begin)],
            send_sem=send_sem,
            recv_sem=recv_sem.at[region, index, part],
            device_id=(following, next_band),
            device_id_type=MESH,
        )

    def arrived(which, index, part):
        begin, end = SPLITS[part]
        landed = incoming.at[which, index, pl.ds(begin, end - begin)]
        pltpu.make_async_copy(landed, landed, recv_sem.at[which, index, part]).wait()

    def pass_on():
        def one(index, carry):
            for part, (begin, end) in enumerate(SPLITS):
                arrived(1, index, part)
                pltpu.make_async_remote_copy(
                    src_ref=incoming.at[1, index, pl.ds(begin, end - begin)],
                    dst_ref=incoming.at[0, index, pl.ds(begin, end - begin)],
                    send_sem=relay_sem,
                    recv_sem=recv_sem.at[0, index, part],
                    device_id=(relay_target, band),
                    device_id_type=MESH,
                ).start()
            return carry

        lax.fori_loop(0, groups, one, 0)
        pltpu.make_async_copy(outgoing, outgoing, relay_sem).wait()

    @pl.when(is_relay & (level >= detour))
    def _():
        pass_on()

    def one_group(index, carry):
        @pl.when(level > 0)
        def _():
            for part in range(len(SPLITS)):
                arrived(0, index, part)

        high, low = split(incoming[0, index])
        pieces[...] = jnp.concatenate([high, low], axis=1)
        for r in range(blocks):
            left = jnp.concatenate([pieces[columns[j, 0, r]] for j in range(nnz)], axis=1)
            right = jnp.concatenate(
                [operator[r, :, c].reshape(nnz * LANE, LANE) for c in range(2)], axis=1
            )
            product = jnp.dot(left, right, preferred_element_type=jnp.float32)
            product = product[:rows] + product[rows:]
            turned = pltpu.roll(product[:, LANE:], half, 0)
            value = product[:, :LANE] + sign * turned
            if r == 0:
                value = value * first_edge
            if r == blocks - 1:
                value = value * last_edge
            outgoing[index, r] = value
            for part, (begin, end) in enumerate(SPLITS):
                if r + 1 == end:
                    to_next(index, part).start()
        return carry

    lax.fori_loop(0, groups, one_group, 0)

    is_source = lax.rem(sublane, 4) < 2
    half_rows = groups // 2 * rows

    def one_pair(index):
        left = outgoing[:, pairs[0, 0, index]].reshape(groups // 2, 2, rows, LANE)
        right = outgoing[:, pairs[0, 1, index]].reshape(groups // 2, 2, rows, LANE)
        lower = jnp.concatenate([left[:, 1, 6:], left[:, 1, :6]], axis=1)
        upper = jnp.concatenate([right[:, 0, 2:], right[:, 0, :2]], axis=1)
        left = jnp.where(is_source[None], left[:, 0], lower)
        right = jnp.where(is_source[None], upper, right[:, 1])
        left_high, left_low = split(left.reshape(half_rows, LANE))
        right_high, right_low = split(right.reshape(half_rows, LANE))
        left_all = jnp.concatenate([left_high, left_high, left_low], axis=0)
        right_all = jnp.concatenate([right_high, right_low, right_high], axis=0)
        term = lax.dot_general(
            left_all, right_all, (((0,), (0,)), ((), ())), preferred_element_type=jnp.float32
        )
        partial[index] = term * scale

    sends = []
    for slot, step in enumerate((2, 3, 1, 0)):
        peer = lax.rem(band + step, bands)
        for pair in range(own_pairs):
            one_pair(peer * own_pairs + pair)
            if step == 0:
                continue
            send = pltpu.make_async_remote_copy(
                src_ref=partial.at[peer * own_pairs + pair],
                dst_ref=gathered.at[slot, pair],
                send_sem=part_send_sem.at[slot, pair],
                recv_sem=part_recv_sem.at[slot, pair],
                device_id=(level, peer),
                device_id_type=MESH,
            )
            send.start()
            sends.append(send)
    for send in sends:
        send.wait_recv()
    total = partial[pl.ds(band * own_pairs, own_pairs)]
    for slot in range(bands - 1):
        total = total + gathered[slot]
    image[0] = total
    for send in sends:
        send.wait_send()
    pltpu.make_async_copy(outgoing, outgoing, send_sem).wait()

    @pl.when(is_relay & (level < detour))
    def _():
        pass_on()

    @pl.when(level == levels - 1)
    def _():
        def drain(index, carry):
            for part in range(len(SPLITS)):
                arrived(2, index, part)
            return carry

        lax.fori_loop(0, groups, drain, 0)


def shards(source_field, receiver_data, propagator, block_columns, image_pairs):
    levels = lax.axis_size("depth")
    bands = lax.axis_size("freq")
    shots, lateral = source_field.shape[2:]
    blocks, nnz = propagator.shape[2:4]
    pair_count = image_pairs.shape[1]
    own_pairs = pair_count // bands
    groups = shots // GROUP
    rows = 4 * GROUP
    scale = 1.0 / math.sqrt(2.0 * shots * bands)
    tile = (LANE, LANE)
    anywhere = pl.BlockSpec(memory_space=pl.ANY)
    return pl.pallas_call(
        functools.partial(kernel, levels, bands, scale),
        out_shape=jax.ShapeDtypeStruct((1, own_pairs) + tile, jnp.float32),
        in_specs=[anywhere] * 5,
        out_specs=pl.BlockSpec(memory_space=pltpu.VMEM),
        scratch_shapes=[
            pltpu.SMEM((nnz, 1, blocks), jnp.int32),
            pltpu.SMEM((1, 2, pair_count), jnp.int32),
            pltpu.VMEM((blocks, nnz, 2) + tile, jnp.bfloat16),
            pltpu.VMEM((2, 2, shots, lateral), jnp.float32),
            pltpu.VMEM((3, groups, blocks, rows, LANE), jnp.float32),
            pltpu.VMEM((groups, blocks, rows, LANE), jnp.float32),
            pltpu.VMEM((blocks, 2 * rows, LANE), jnp.bfloat16),
            pltpu.VMEM((pair_count,) + tile, jnp.float32),
            pltpu.VMEM((bands - 1, own_pairs) + tile, jnp.float32),
            pltpu.SemaphoreType.DMA((5,)),
            pltpu.SemaphoreType.DMA,
            pltpu.SemaphoreType.DMA,
            pltpu.SemaphoreType.DMA((3, groups, len(SPLITS))),
            pltpu.SemaphoreType.DMA((bands - 1, own_pairs)),
            pltpu.SemaphoreType.DMA((bands - 1, own_pairs)),
        ],
        compiler_params=pltpu.CompilerParams(
            collective_id=0,
            has_side_effects=True,
            vmem_limit_bytes=63 * 2**20,
        ),
    )(
        jnp.transpose(block_columns, (2, 0, 1)),
        jnp.transpose(image_pairs, (0, 2, 1)),
        source_field,
        receiver_data,
        propagator,
    )


def solution(mesh):
    placed = (
        P("freq", None, None, None),
        P("freq", None, None, None),
        P("freq", "depth", None, None, None, None, None),
        P("depth", None, None),
        P("depth", None, None),
    )
    return jax.shard_map(
        shards,
        mesh=mesh,
        in_specs=placed,
        out_specs=P("depth", "freq", None, None),
        check_vma=False,
    )
```

```python
import functools
import math

import jax
import jax.numpy as jnp
from jax import lax
from jax.experimental import pallas as pl
from jax.experimental.pallas import tpu as pltpu
from jax.sharding import PartitionSpec as P

GROUP = 2
SPLITS = ((0, 4), (4, 8), (8, 12), (12, 16))
LAG = 2
RUN = 4
PLANE = 16
SIDES = 32
LANE = 128
MESH = pl.DeviceIdType.MESH


def split(value):
    high = value.astype(jnp.bfloat16)
    low = (value - high.astype(jnp.float32)).astype(jnp.bfloat16)
    return high, low


def edge_row(last_block):
    lane = lax.broadcasted_iota(jnp.int32, (1, LANE), 1)
    distance = LANE - 1 - lane if last_block else lane
    ramp = jnp.maximum(0.0, 1.0 - distance.astype(jnp.float32) / 64.0)
    return 1.0 - 0.3 * ramp * ramp


def kernel(
    levels, bands, scale,
    columns_hbm, pairs_hbm, source_hbm, receiver_hbm, operator_hbm,
    image,
    columns, pairs, operator, surface, incoming, outgoing, pieces, partial, gathered,
    load_sem, send_sem, relay_sem, recv_sem, part_send_sem, part_recv_sem,
):
    level = lax.axis_index("depth")
    band = lax.axis_index("freq")
    last = level // (levels - 1)
    side_core = lax.rem(band, 2)
    relayed = side_core * (lax.rem(level, RUN) // (RUN - 1)) * (1 - last)
    region = relayed + 2 * last
    detour = PLANE - RUN + 1 + SIDES * (band // 2)
    following = lax.rem(level + 1 + (detour - 1) * relayed, levels)
    following = following + last * (levels - 1)
    next_band = band + last * (1 - 2 * side_core)
    relay_target = lax.rem(level + levels + 1 - detour, levels)
    is_relay = (side_core == 1) & (lax.rem(level, RUN) == 0) & (level != detour - 1)
    groups = outgoing.shape[0]
    blocks = outgoing.shape[1]
    rows = outgoing.shape[2]
    half = rows // 2
    nnz = operator.shape[1]
    own_pairs = image.shape[1]

    loads = [
        pltpu.make_async_copy(source_hbm.at[0], surface.at[0], load_sem.at[0]),
        pltpu.make_async_copy(receiver_hbm.at[0], surface.at[1], load_sem.at[1]),
        pltpu.make_async_copy(operator_hbm.at[0, 0], operator, load_sem.at[2]),
        pltpu.make_async_copy(columns_hbm, columns, load_sem.at[3]),
        pltpu.make_async_copy(pairs_hbm, pairs, load_sem.at[4]),
    ]
    for load in loads:
        load.start()

    barrier = pltpu.get_barrier_semaphore()
    distances = [1, detour, detour - 1]
    for distance in distances:
        for step in (distance, levels - distance):
            pl.semaphore_signal(
                barrier,
                inc=1,
                device_id=(lax.rem(level + step, levels), band),
                device_id_type=MESH,
            )
    for step in range(1, bands):
        peer = lax.rem(band + step, bands)
        pl.semaphore_signal(barrier, inc=1, device_id=(level, peer), device_id_type=MESH)
    pl.semaphore_wait(barrier, 2 * len(distances) + bands - 1)
    for load in loads:
        load.wait()

    sublane = lax.broadcasted_iota(jnp.int32, (8, LANE), 0)

    def fill(tile):
        shots = pl.ds(pl.multiple_of(tile * 8, 8), 8)
        for block in range(blocks):
            lanes = pl.ds(block * LANE, LANE)
            parts = [
                surface[0, 0, shots, lanes],
                surface[1, 0, shots, lanes],
                surface[0, 1, shots, lanes],
                surface[1, 1, shots, lanes],
            ]
            for q in range(4):
                made = parts[0] if q == 0 else pltpu.roll(parts[0], (8 - 2 * q) % 8, 0)
                for m in range(1, 4):
                    shift = (2 * (m - q)) % 8
                    moved = parts[m] if shift == 0 else pltpu.roll(parts[m], shift, 0)
                    made = jnp.where(sublane >= 2 * m, moved, made)
                incoming[0, tile * 4 + q, block] = made

    @pl.when(level == 0)
    def _():
        def one_tile(tile, carry):
            fill(tile)
            return carry

        lax.fori_loop(0, groups // 4, one_tile, 0)

    sign = jnp.where((sublane < 2) | (sublane >= 6), -1.0, 1.0).astype(jnp.float32)
    first_edge = edge_row(False)
    last_edge = edge_row(True)

    def to_next(index, part):
        begin, end = SPLITS[part]
        return pltpu.make_async_remote_copy(
            src_ref=outgoing.at[index, pl.ds(begin, end - begin)],
            dst_ref=incoming.at[region, index, pl.ds(begin, end - begin)],
            send_sem=send_sem,
            recv_sem=recv_sem.at[region, index, part],
            device_id=(following, next_band),
            device_id_type=MESH,
        )

    def arrived(which, index, part):
        begin, end = SPLITS[part]
        landed = incoming.at[which, index, pl.ds(begin, end - begin)]
        pltpu.make_async_copy(landed, landed, recv_sem.at[which, index, part]).wait()

    def pass_on():
        def one(index, carry):
            for part, (begin, end) in enumerate(SPLITS):
                arrived(1, index, part)
                pltpu.make_async_remote_copy(
                    src_ref=incoming.at[1, index, pl.ds(begin, end - begin)],
                    dst_ref=incoming.at[0, index, pl.ds(begin, end - begin)],
                    send_sem=relay_sem,
                    recv_sem=recv_sem.at[0, index, part],
                    device_id=(relay_target, band),
                    device_id_type=MESH,
                ).start()
            return carry

        lax.fori_loop(0, groups, one, 0)
        pltpu.make_async_copy(outgoing, outgoing, relay_sem).wait()

    @pl.when(is_relay & (level >= detour))
    def _():
        pass_on()

    def one_group(index, carry):
        @pl.when(level > 0)
        def _():
            for part in range(len(SPLITS)):
                arrived(0, index, part)

        high, low = split(incoming[0, index])
        pieces[...] = jnp.concatenate([high, low], axis=1)
        def multiply(r):
            left = jnp.concatenate([pieces[columns[j, 0, r]] for j in range(nnz)], axis=1)
            right = jnp.concatenate(
                [operator[r, :, c].reshape(nnz * LANE, LANE) for c in range(2)], axis=1
            )
            return jnp.dot(left, right, preferred_element_type=jnp.float32)

        def finish(r, product):
            product = product[:rows] + product[rows:]
            turned = pltpu.roll(product[:, LANE:], half, 0)
            value = product[:, :LANE] + sign * turned
            if r == 0:
                value = value * first_edge
            if r == blocks - 1:
                value = value * last_edge
            outgoing[index, r] = value
            for part, (begin, end) in enumerate(SPLITS):
                if r + 1 == end:
                    to_next(index, part).start()

        products = {}
        for r in range(blocks + LAG):
            if r < blocks:
                products[r] = multiply(r)
            if r >= LAG:
                finish(r - LAG, products.pop(r - LAG))
        return carry

    lax.fori_loop(0, groups, one_group, 0)

    is_source = lax.rem(sublane, 4) < 2
    half_rows = groups // 2 * rows

    def one_pair(index):
        left = outgoing[:, pairs[0, 0, index]].reshape(groups // 2, 2, rows, LANE)
        right = outgoing[:, pairs[0, 1, index]].reshape(groups // 2, 2, rows, LANE)
        lower = jnp.concatenate([left[:, 1, 6:], left[:, 1, :6]], axis=1)
        upper = jnp.concatenate([right[:, 0, 2:], right[:, 0, :2]], axis=1)
        left = jnp.where(is_source[None], left[:, 0], lower)
        right = jnp.where(is_source[None], upper, right[:, 1])
        left_high, left_low = split(left.reshape(half_rows, LANE))
        right_high, right_low = split(right.reshape(half_rows, LANE))
        left_all = jnp.concatenate([left_high, left_high, left_low], axis=0)
        right_all = jnp.concatenate([right_high, right_low, right_high], axis=0)
        term = lax.dot_general(
            left_all, right_all, (((0,), (0,)), ((), ())), preferred_element_type=jnp.float32
        )
        partial[index] = term * scale

    sends = []
    for slot, step in enumerate((2, 3, 1, 0)):
        peer = lax.rem(band + step, bands)
        for pair in range(own_pairs):
            one_pair(peer * own_pairs + pair)
            if step == 0:
                continue
            send = pltpu.make_async_remote_copy(
                src_ref=partial.at[peer * own_pairs + pair],
                dst_ref=gathered.at[slot, pair],
                send_sem=part_send_sem.at[slot, pair],
                recv_sem=part_recv_sem.at[slot, pair],
                device_id=(level, peer),
                device_id_type=MESH,
            )
            send.start()
            sends.append(send)
    for send in sends:
        send.wait_recv()
    total = partial[pl.ds(band * own_pairs, own_pairs)]
    for slot in range(bands - 1):
        total = total + gathered[slot]
    image[0] = total
    for send in sends:
        send.wait_send()
    pltpu.make_async_copy(outgoing, outgoing, send_sem).wait()

    @pl.when(is_relay & (level < detour))
    def _():
        pass_on()

    @pl.when(level == levels - 1)
    def _():
        def drain(index, carry):
            for part in range(len(SPLITS)):
                arrived(2, index, part)
            return carry

        lax.fori_loop(0, groups, drain, 0)


def shards(source_field, receiver_data, propagator, block_columns, image_pairs):
    levels = lax.axis_size("depth")
    bands = lax.axis_size("freq")
    shots, lateral = source_field.shape[2:]
    blocks, nnz = propagator.shape[2:4]
    pair_count = image_pairs.shape[1]
    own_pairs = pair_count // bands
    groups = shots // GROUP
    rows = 4 * GROUP
    scale = 1.0 / math.sqrt(2.0 * shots * bands)
    tile = (LANE, LANE)
    anywhere = pl.BlockSpec(memory_space=pl.ANY)
    return pl.pallas_call(
        functools.partial(kernel, levels, bands, scale),
        out_shape=jax.ShapeDtypeStruct((1, own_pairs) + tile, jnp.float32),
        in_specs=[anywhere] * 5,
        out_specs=pl.BlockSpec(memory_space=pltpu.VMEM),
        scratch_shapes=[
            pltpu.SMEM((nnz, 1, blocks), jnp.int32),
            pltpu.SMEM((1, 2, pair_count), jnp.int32),
            pltpu.VMEM((blocks, nnz, 2) + tile, jnp.bfloat16),
            pltpu.VMEM((2, 2, shots, lateral), jnp.float32),
            pltpu.VMEM((3, groups, blocks, rows, LANE), jnp.float32),
            pltpu.VMEM((groups, blocks, rows, LANE), jnp.float32),
            pltpu.VMEM((blocks, 2 * rows, LANE), jnp.bfloat16),
            pltpu.VMEM((pair_count,) + tile, jnp.float32),
            pltpu.VMEM((bands - 1, own_pairs) + tile, jnp.float32),
            pltpu.SemaphoreType.DMA((5,)),
            pltpu.SemaphoreType.DMA,
            pltpu.SemaphoreType.DMA,
            pltpu.SemaphoreType.DMA((3, groups, len(SPLITS))),
            pltpu.SemaphoreType.DMA((bands - 1, own_pairs)),
            pltpu.SemaphoreType.DMA((bands - 1, own_pairs)),
        ],
        compiler_params=pltpu.CompilerParams(
            collective_id=0,
            has_side_effects=True,
            vmem_limit_bytes=63 * 2**20,
        ),
    )(
        jnp.transpose(block_columns, (2, 0, 1)),
        jnp.transpose(image_pairs, (0, 2, 1)),
        source_field,
        receiver_data,
        propagator,
    )


def solution(mesh):
    placed = (
        P("freq", None, None, None),
        P("freq", None, None, None),
        P("freq", "depth", None, None, None, None, None),
        P("depth", None, None),
        P("depth", None, None),
    )
    return jax.shard_map(
        shards,
        mesh=mesh,
        in_specs=placed,
        out_specs=P("depth", "freq", None, None),
        check_vma=False,
    )
```
